32 devices in a mesh: gx: 8 (over z, y), gy: 4 (over x, core).
Axes of the slice: x: 2, y: 2, z: 4, core: 2. Of those that a mesh axis runs over, the one named last changes fastest.
Arguments:
- fuel: float32 [16, 768, 384], P('gx', 'gy'), may hold values from -41 to 41, as said below
- oxidizer: float32 [16, 768, 384], P('gx', 'gy'), may hold values from -41 to 41, as said below
- kappa: float32 [16, 768, 384], P('gx', 'gy'), may hold values from 0.05 to 0.5
- rate: float32 [16, 768, 384], P('gx', 'gy'), may hold values from 0.5 to 5
Outputs:
- fuel_next: float32 [16, 768, 384], P('gx', 'gy')
- oxid_next: float32 [16, 768, 384], P('gx', 'gy')
- r_factor: float32 [384, 384], replicated
The draws below stay inside these ranges and needn't reach their ends.
Inputs may be any that keep to these rules, and one draw needn't show every extreme that they name: `fuel`: A real-valued field. `oxidizer`: A real-valued field.
All inputs are finite; a program needn't handle non-finite values.
Results may differ from the reference program's by a relative error of at most 0.000067.
Values sent between devices are 32-bit elements; how exact they have to be, the bound alone decides.
A program may use at most 64 MiB of HBM per device.

```python
import math
import jax
import jax.numpy as jnp
from jax import lax

NZ = 384
NX = 16
NY = 768


def field_draw(key, salt):
    key = jax.random.fold_in(key, salt)
    keys = jax.random.split(key, 5)
    ramp = jnp.arange(NX, dtype=jnp.float32) / max(NX - 1, 1)
    row_scale = jnp.exp(jax.random.uniform(keys[0], (NX, NY), jnp.float32, math.log(0.5), math.log(1.5)))
    row_scale = row_scale * (0.5 + ramp)[:, None]
    col_scale = jnp.exp(jax.random.uniform(keys[1], (NZ,), jnp.float32, math.log(0.3), math.log(3.0)))
    profile = jax.random.uniform(keys[2], (NZ,), jnp.float32, -1.0, 1.0)
    noise = jnp.clip(jax.random.normal(keys[3], (NX, NY, NZ), jnp.float32), -3.0, 3.0)
    common = jnp.clip(jax.random.normal(keys[4], (NX, NY), jnp.float32), -3.0, 3.0)
    inner = noise + common[:, :, None] * profile[None, None, :]
    return (row_scale[:, :, None] * col_scale[None, None, :] * inner).astype(jnp.float32)


def draw_fuel(key, part):
    return field_draw(key, 11)


def draw_oxidizer(key, part):
    return field_draw(key, 23)


def levels(stream_key, extent, shards, smallest, largest):
    factor_of, own = 1.0, jax.random.fold_in(stream_key, 6)
    for position, parts in shards:
        steps = jnp.exp(jax.random.uniform(jax.random.fold_in(own, position), (parts,), jnp.float32, smallest / len(shards), largest / len(shards)))
        factor_of = factor_of * jnp.repeat(steps, extent[position] // parts).reshape([-1 if axis == position else 1 for axis in range(len(extent))])
    return factor_of


def setup_inputs(seed: int = 0) -> dict:
    key_of = jax.random.split(jax.random.key(seed), 5)
    fuel = draw_fuel(jax.random.fold_in(key_of[4], 71), 0)
    oxidizer = draw_oxidizer(jax.random.fold_in(key_of[4], 71), 0)
    kappa = jnp.clip(0.05 + 0.45 * jax.random.uniform(key_of[2], (NX, NY, NZ), jnp.float32) ** levels(key_of[2], (NX, NY, NZ), ((0, 8), (1, 4)), -0.2, 0.2), 0.05, 0.5)
    rate = jnp.clip(jnp.exp(math.log(5.0) - 2.3025851 * jax.random.uniform(key_of[3], (NX, NY, NZ), jnp.float32) ** levels(key_of[3], (NX, NY, NZ), ((0, 8), (1, 4)), -0.2, 0.2)), 0.5, 5.0)
    return {"fuel": fuel, "oxidizer": oxidizer, "kappa": kappa, "rate": rate}


def diffuse(field, kappa):
    padded = jnp.pad(field, 1)
    kpad = jnp.pad(kappa, 1)
    total = jnp.zeros_like(field)
    center = padded[1:-1, 1:-1, 1:-1]
    kcenter = kpad[1:-1, 1:-1, 1:-1]
    for axis in range(3):
        for offset in (0, 2):
            index = [slice(1, -1)] * 3
            index[axis] = slice(offset, offset + field.shape[axis])
            index = tuple(index)
            total = total + 0.5 * (kcenter + kpad[index]) * (padded[index] - center)
    return total

def reference(fuel, oxidizer, kappa, rate):
    prod = fuel * oxidizer
    react = rate * prod / jnp.sqrt(1.0 + prod * prod)
    fuel_next = fuel + 0.15 * (diffuse(fuel, kappa) - react)
    oxid_next = oxidizer + 0.15 * (diffuse(oxidizer, kappa) + react)
    rows = 2 * fuel.shape[0] * fuel.shape[1]
    flat_a = fuel_next.reshape(-1, fuel.shape[2])
    flat_b = oxid_next.reshape(-1, fuel.shape[2])
    dims = (((0,), (0,)), ((), ()))
    gram = lax.dot_general(flat_a, flat_a, dims, precision=lax.Precision.HIGHEST)
    gram = gram + lax.dot_general(flat_b, flat_b, dims, precision=lax.Precision.HIGHEST)
    gram = gram / rows
    lower = jnp.linalg.cholesky(gram)
    return (fuel_next, oxid_next, lower.T)
```

```python
import functools

import jax
import jax.numpy as jnp
from jax import lax
from jax.experimental import pallas as pl
from jax.experimental.pallas import tpu as pltpu
from jax.sharding import PartitionSpec as P

MESH = pl.DeviceIdType.MESH
TILE = 8
LANES = 128
HIGHEST = lax.Precision.HIGHEST


def halo_kernel(n, m, f_ref, o_ref, k_ref, xlo, xhi, ylo, yhi, send_sem, recv_sem):
    i, j = lax.axis_index("gx"), lax.axis_index("gy")
    planes, width = f_ref.shape[0], f_ref.shape[1]
    sides = (
        (i < n - 1, i > 0, i + 1, j),
        (i > 0, i < n - 1, i - 1, j),
        (j < m - 1, j > 0, i, j + 1),
        (j > 0, j < m - 1, i, j - 1),
    )
    barrier = pltpu.get_barrier_semaphore()
    for has, _, a, b in sides:
        @pl.when(has)
        def _(a=a, b=b):
            pl.semaphore_signal(barrier, inc=1, device_id=(a, b), device_id_type=MESH)
    pl.semaphore_wait(barrier, sum(has.astype(jnp.int32) for has, _, _, _ in sides))
    outs = (xlo, xhi, ylo, yhi)

    def copies(side, a, b):
        made = []
        for t, ref in enumerate((f_ref, o_ref, k_ref)):
            src = (
                ref.at[planes - 1],
                ref.at[0],
                ref.at[:, pl.ds(width - TILE, TILE)],
                ref.at[:, pl.ds(0, TILE)],
            )[side]
            made.append(
                pltpu.make_async_remote_copy(
                    src_ref=src,
                    dst_ref=outs[side].at[t],
                    send_sem=send_sem.at[side, t],
                    recv_sem=recv_sem.at[side, t],
                    device_id=(a, b),
                    device_id_type=MESH,
                )
            )
        return made

    for side, (has, _, a, b) in enumerate(sides):
        @pl.when(has)
        def _(side=side, a=a, b=b):
            for copy in copies(side, a, b):
                copy.start()
    for side, (has, gets, a, b) in enumerate(sides):
        @pl.when(has)
        def _(side=side, a=a, b=b):
            for copy in copies(side, a, b):
                copy.wait_send()

        @pl.when(gets)
        def _(side=side, a=a, b=b):
            for copy in copies(side, a, b):
                copy.wait_recv()


def halo(n, m, fuel, oxidizer, kappa):
    planes, width, depth = fuel.shape
    any_spec = pl.BlockSpec(memory_space=pl.ANY)
    xs = jax.ShapeDtypeStruct((3, width, depth), jnp.float32)
    ys = jax.ShapeDtypeStruct((3, planes, TILE, depth), jnp.float32)
    return pl.pallas_call(
        functools.partial(halo_kernel, n, m),
        out_shape=(xs, xs, ys, ys),
        in_specs=[any_spec] * 3,
        out_specs=(any_spec,) * 4,
        scratch_shapes=[pltpu.SemaphoreType.DMA((4, 3)), pltpu.SemaphoreType.DMA((4, 3))],
        compiler_params=pltpu.CompilerParams(collective_id=0, has_side_effects=True),
        name="halo",
    )(fuel, oxidizer, kappa)


def stencil_kernel(n, m, rows, step, f_ref, o_ref, k_ref, r_ref, xlo, xhi, ylo, yhi, fn_ref, on_ref, g_ref):
    i, j = lax.axis_index("gx"), lax.axis_index("gy")
    planes, width, depth = f_ref.shape
    row = lax.broadcasted_iota(jnp.int32, (step, depth), 0)
    lane = lax.broadcasted_iota(jnp.int32, (step, depth), 1)
    refs = (f_ref, o_ref, k_ref)
    zero = jnp.zeros((step, depth), jnp.float32)
    zrow = jnp.zeros((1, depth), jnp.float32)
    for x in range(planes):
        for y in range(0, width, step):
            part = pl.ds(y, step)
            center = [ref[x, part] for ref in refs]
            sets = []
            if x == 0:
                sets.append([jnp.where(i > 0, xlo[t, part], zero) for t in range(3)])
            else:
                sets.append([ref[x - 1, part] for ref in refs])
            if x == planes - 1:
                sets.append([jnp.where(i < n - 1, xhi[t, part], zero) for t in range(3)])
            else:
                sets.append([ref[x + 1, part] for ref in refs])
            if y == 0:
                before = [jnp.where(j > 0, ylo[t, x, TILE - 1:TILE], zrow) for t in range(3)]
            else:
                before = [ref[x, y - 1:y] for ref in refs]
            if y + step == width:
                after = [jnp.where(j < m - 1, yhi[t, x, 0:1], zrow) for t in range(3)]
            else:
                after = [ref[x, y + step:y + step + 1] for ref in refs]
            sets.append([jnp.where(row == 0, b, pltpu.roll(c, 1, 0)) for b, c in zip(before, center)])
            sets.append([jnp.where(row == step - 1, a, pltpu.roll(c, step - 1, 0)) for a, c in zip(after, center)])
            sets.append([jnp.where(lane == 0, 0.0, pltpu.roll(c, 1, 1)) for c in center])
            sets.append([jnp.where(lane == depth - 1, 0.0, pltpu.roll(c, depth - 1, 1)) for c in center])
            fc, oc, kc = center
            df, do = zero, zero
            for fs, os, ks in sets:
                weight = 0.5 * (kc + ks)
                df = df + weight * (fs - fc)
                do = do + weight * (os - oc)
            prod = fc * oc
            react = r_ref[x, part] * prod / jnp.sqrt(1.0 + prod * prod)
            fn_ref[x, part] = fc + 0.15 * (df - react)
            on_ref[x, part] = oc + 0.15 * (do + react)
    dims = (((0,), (0,)), ((), ()))
    at = 0
    flat = [ref[...].reshape(planes * width, depth) for ref in (fn_ref, on_ref)]
    for a in range(0, depth, LANES):
        total = sum(
            lax.dot_general(u[:, a:a + LANES], u[:, a:], dims, precision=HIGHEST, preferred_element_type=jnp.float32)
            for u in flat
        ) / rows
        for b in range(0, depth - a, LANES):
            g_ref[at:at + LANES] = total[:, b:b + LANES]
            at += LANES


def stencil(n, m, rows, fuel, oxidizer, kappa, rate, halos):
    planes, width, depth = fuel.shape
    blocks = depth // LANES
    field = jax.ShapeDtypeStruct(fuel.shape, jnp.float32)
    vmem = pl.BlockSpec(memory_space=pltpu.VMEM)
    return pl.pallas_call(
        functools.partial(stencil_kernel, n, m, rows, 32),
        out_shape=(field, field, jax.ShapeDtypeStruct((blocks * (blocks + 1) // 2 * LANES, LANES), jnp.float32)),
        in_specs=[vmem] * 8,
        out_specs=(vmem,) * 3,
        name="stencil",
    )(fuel, oxidizer, kappa, rate, *halos)


def sum_kernel(stages, g_ref, out_ref, *scratch):
    count = len(stages)
    inbox, held, sems = scratch[:count], scratch[count:2 * count], scratch[2 * count:]
    index = {"gx": lax.axis_index("gx"), "gy": lax.axis_index("gy")}

    def peer(stage, k):
        axis, stride, size = stage
        mine = lax.rem(index[axis] // stride, size)
        other = lax.rem(mine + k, size)
        place = dict(index)
        place[axis] = index[axis] + (other - mine) * stride
        return mine, other, (place["gx"], place["gy"])

    barrier = pltpu.get_barrier_semaphore()
    greeted = 0
    for stage in stages:
        for k in range(1, stage[2]):
            pl.semaphore_signal(barrier, inc=1, device_id=peer(stage, k)[2], device_id_type=MESH)
            greeted += 1
    pl.semaphore_wait(barrier, greeted)
    source = g_ref
    length = g_ref.shape[0]
    starts = []
    start = 0
    for s, stage in enumerate(stages):
        size = stage[2]
        length //= size
        sent = []
        for k in range(1, size):
            mine, other, device = peer(stage, k)
            sent.append(
                pltpu.make_async_remote_copy(
                    src_ref=source.at[pl.ds(pl.multiple_of(other * length, TILE), length)],
                    dst_ref=inbox[s].at[k - 1],
                    send_sem=sems[0].at[s, k - 1],
                    recv_sem=sems[1].at[s, k - 1],
                    device_id=device,
                    device_id_type=MESH,
                )
            )
            sent[-1].start()
        for copy in sent:
            copy.wait_recv()
        total = source[pl.ds(pl.multiple_of(mine * length, TILE), length)]
        for k in range(1, size):
            total = total + inbox[s][k - 1]
        held[s][...] = total
        for copy in sent:
            copy.wait_send()
        source = held[s]
        start = start + mine * length
        starts.append((start, length))
    part = pl.ds(pl.multiple_of(start, TILE), length)
    out_ref[part] = source[...]
    for s in reversed(range(count)):
        stage = stages[s]
        start, length = starts[s]
        part = pl.ds(pl.multiple_of(start, TILE), length)
        sent = []
        for k in range(1, stage[2]):
            sent.append(
                pltpu.make_async_remote_copy(
                    src_ref=out_ref.at[part],
                    dst_ref=out_ref.at[part],
                    send_sem=sems[2].at[s, k - 1],
                    recv_sem=sems[3].at[s, k - 1],
                    device_id=peer(stage, k)[2],
                    device_id_type=MESH,
                )
            )
            sent[-1].start()
        for copy in sent:
            copy.wait()


def sum_over_all(stages, gram):
    length, lanes = gram.shape
    inbox, held = [], []
    most = max(stage[2] for stage in stages)
    for _, _, size in stages:
        length //= size
        inbox.append(pltpu.VMEM((size - 1, length, lanes), jnp.float32))
        held.append(pltpu.VMEM((length, lanes), jnp.float32))
    vmem = pl.BlockSpec(memory_space=pltpu.VMEM)
    return pl.pallas_call(
        functools.partial(sum_kernel, stages),
        out_shape=jax.ShapeDtypeStruct(gram.shape, jnp.float32),
        in_specs=[vmem],
        out_specs=vmem,
        scratch_shapes=[*inbox, *held] + [pltpu.SemaphoreType.DMA((len(stages), most - 1))] * 4,
        compiler_params=pltpu.CompilerParams(collective_id=1, has_side_effects=True),
        name="allsum",
    )(gram)


def factor_kernel(g_ref, r_ref, a_ref):
    depth = r_ref.shape[0]
    blocks = depth // LANES
    at = 0
    for b in range(blocks):
        for c in range(b, blocks):
            a_ref[b * LANES:(b + 1) * LANES, c * LANES:(c + 1) * LANES] = g_ref[at:at + LANES]
            at += LANES
    dims = (((0,), (0,)), ((), ()))
    dot = functools.partial(lax.dot_general, dimension_numbers=dims, precision=HIGHEST, preferred_element_type=jnp.float32)
    for b in range(blocks):
        c0 = b * LANES
        wide = depth - c0
        sub = lax.broadcasted_iota(jnp.int32, (TILE, wide), 0)
        lane = lax.broadcasted_iota(jnp.int32, (TILE, wide), 1)
        if c0:
            r_ref[c0:c0 + LANES, :c0] = jnp.zeros((LANES, c0), jnp.float32)
        for p in range(0, LANES, TILE):
            r0 = c0 + p
            panel = a_ref[r0:r0 + TILE, c0:]
            e = {}
            for k in range(TILE):
                column = jnp.broadcast_to(panel[:, p + k:p + k + 1], (TILE, LANES))
                for i in range(k, TILE):
                    e[i, k] = jnp.broadcast_to(column[i:i + 1], (TILE, LANES))
            inv, low = [], {}
            for k in range(TILE):
                inv.append(lax.rsqrt(e[k, k]))
                for i in range(k + 1, TILE):
                    low[i, k] = e[i, k] * inv[k]
                for j in range(k + 1, TILE):
                    for i in range(j, TILE):
                        e[i, j] = e[i, j] - low[i, k] * low[j, k]
            done = [[] for _ in range(TILE)]
            strips = []
            for c in range(0, wide, LANES):
                rows = []
                for k in range(TILE):
                    value = jnp.broadcast_to(panel[k:k + 1, c:c + LANES], (TILE, LANES))
                    for j in range(k):
                        value = value - low[k, j] * rows[j]
                    rows.append(value * inv[k])
                strip = rows[0]
                for k in range(1, TILE):
                    strip = jnp.where(sub[:, :LANES] == k, rows[k], strip)
                strips.append(strip)
            strips[0] = jnp.where(lane[:, :LANES] >= sub[:, :LANES] + p, strips[0], 0.0)
            upper = strips[0] if len(strips) == 1 else jnp.concatenate(strips, axis=1)
            r_ref[r0:r0 + TILE, c0:] = upper
            if p + TILE < LANES:
                change = dot(upper[:, :LANES], upper)
                a_ref[r0 + TILE:c0 + LANES, c0:] -= change[p + TILE:]
        for d in range(b + 1, blocks):
            d0 = d * LANES
            a_ref[d0:d0 + LANES, d0:] -= dot(r_ref[c0:c0 + LANES, d0:d0 + LANES], r_ref[c0:c0 + LANES, d0:])


def factor(gram, depth):
    vmem = pl.BlockSpec(memory_space=pltpu.VMEM)
    return pl.pallas_call(
        factor_kernel,
        out_shape=jax.ShapeDtypeStruct((depth, depth), jnp.float32),
        in_specs=[vmem],
        out_specs=vmem,
        scratch_shapes=[pltpu.VMEM((depth, depth), jnp.float32)],
        name="factor",
    )(gram)


def shards(n, m, fuel, oxidizer, kappa, rate):
    planes, width, depth = fuel.shape
    rows = 2 * planes * width * n * m
    halos = halo(n, m, fuel, oxidizer, kappa)
    fuel_next, oxid_next, gram = stencil(n, m, rows, fuel, oxidizer, kappa, rate, halos)
    pairs = [("gy", 1, 2), ("gy", 2, 2)] if m == 4 else [("gy", 1, m)]
    stages = tuple(pairs + [("gx", 1, n)])
    if gram.shape[0] % (TILE * n * m) == 0:
        gram = sum_over_all(stages, gram)
    else:
        gram = lax.psum(gram, ("gx", "gy"))
    return (fuel_next, oxid_next, factor(gram, depth))


def solution(mesh):
    spec = P("gx", "gy", None)
    body = functools.partial(shards, mesh.shape["gx"], mesh.shape["gy"])
    return jax.shard_map(body, mesh=mesh, in_specs=(spec,) * 4, out_specs=(spec, spec, P()), check_vma=False)
```

```python
import functools

import jax
import jax.numpy as jnp
from jax import lax
from jax.experimental import pallas as pl
from jax.experimental.pallas import tpu as pltpu
from jax.sharding import PartitionSpec as P

MESH = pl.DeviceIdType.MESH
TILE = 8
LANES = 128
HIGHEST = lax.Precision.HIGHEST


def halo_kernel(n, m, f_ref, o_ref, k_ref, xlo, xhi, ylo, yhi, send_sem, recv_sem):
    i, j = lax.axis_index("gx"), lax.axis_index("gy")
    planes, width = f_ref.shape[0], f_ref.shape[1]
    sides = (
        (i < n - 1, i > 0, i + 1, j),
        (i > 0, i < n - 1, i - 1, j),
        (j < m - 1, j > 0, i, j + 1),
        (j > 0, j < m - 1, i, j - 1),
    )
    barrier = pltpu.get_barrier_semaphore()
    for has, _, a, b in sides:
        @pl.when(has)
        def _(a=a, b=b):
            pl.semaphore_signal(barrier, inc=1, device_id=(a, b), device_id_type=MESH)
    pl.semaphore_wait(barrier, sum(has.astype(jnp.int32) for has, _, _, _ in sides))
    outs = (xlo, xhi, ylo, yhi)

    def copies(side, a, b):
        made = []
        for t, ref in enumerate((f_ref, o_ref, k_ref)):
            src = (
                ref.at[planes - 1],
                ref.at[0],
                ref.at[:, pl.ds(width - TILE, TILE)],
                ref.at[:, pl.ds(0, TILE)],
            )[side]
            made.append(
                pltpu.make_async_remote_copy(
                    src_ref=src,
                    dst_ref=outs[side].at[t],
                    send_sem=send_sem.at[side, t],
                    recv_sem=recv_sem.at[side, t],
                    device_id=(a, b),
                    device_id_type=MESH,
                )
            )
        return made

    for side, (has, _, a, b) in enumerate(sides):
        @pl.when(has)
        def _(side=side, a=a, b=b):
            for copy in copies(side, a, b):
                copy.start()
    for side, (has, gets, a, b) in enumerate(sides):
        @pl.when(has)
        def _(side=side, a=a, b=b):
            for copy in copies(side, a, b):
                copy.wait_send()

        @pl.when(gets)
        def _(side=side, a=a, b=b):
            for copy in copies(side, a, b):
                copy.wait_recv()


def halo(n, m, fuel, oxidizer, kappa):
    planes, width, depth = fuel.shape
    any_spec = pl.BlockSpec(memory_space=pl.ANY)
    xs = jax.ShapeDtypeStruct((3, width, depth), jnp.float32)
    ys = jax.ShapeDtypeStruct((3, planes, TILE, depth), jnp.float32)
    return pl.pallas_call(
        functools.partial(halo_kernel, n, m),
        out_shape=(xs, xs, ys, ys),
        in_specs=[any_spec] * 3,
        out_specs=(any_spec,) * 4,
        scratch_shapes=[pltpu.SemaphoreType.DMA((4, 3)), pltpu.SemaphoreType.DMA((4, 3))],
        compiler_params=pltpu.CompilerParams(collective_id=0, has_side_effects=True),
        name="halo",
    )(fuel, oxidizer, kappa)


def stencil_kernel(n, m, rows, step, f_ref, o_ref, k_ref, r_ref, xlo, xhi, ylo, yhi, fn_ref, on_ref, g_ref):
    i, j = lax.axis_index("gx"), lax.axis_index("gy")
    planes, width, depth = f_ref.shape
    row = lax.broadcasted_iota(jnp.int32, (step, depth), 0)
    lane = lax.broadcasted_iota(jnp.int32, (step, depth), 1)
    refs = (f_ref, o_ref, k_ref)
    zero = jnp.zeros((step, depth), jnp.float32)
    zrow = jnp.zeros((1, depth), jnp.float32)
    for x in range(planes):
        for y in range(0, width, step):
            part = pl.ds(y, step)
            center = [ref[x, part] for ref in refs]
            sets = []
            if x == 0:
                sets.append([jnp.where(i > 0, xlo[t, part], zero) for t in range(3)])
            else:
                sets.append([ref[x - 1, part] for ref in refs])
            if x == planes - 1:
                sets.append([jnp.where(i < n - 1, xhi[t, part], zero) for t in range(3)])
            else:
                sets.append([ref[x + 1, part] for ref in refs])
            if y == 0:
                before = [jnp.where(j > 0, ylo[t, x, TILE - 1:TILE], zrow) for t in range(3)]
            else:
                before = [ref[x, y - 1:y] for ref in refs]
            if y + step == width:
                after = [jnp.where(j < m - 1, yhi[t, x, 0:1], zrow) for t in range(3)]
            else:
                after = [ref[x, y + step:y + step + 1] for ref in refs]
            sets.append([jnp.where(row == 0, b, pltpu.roll(c, 1, 0)) for b, c in zip(before, center)])
            sets.append([jnp.where(row == step - 1, a, pltpu.roll(c, step - 1, 0)) for a, c in zip(after, center)])
            sets.append([jnp.where(lane == 0, 0.0, pltpu.roll(c, 1, 1)) for c in center])
            sets.append([jnp.where(lane == depth - 1, 0.0, pltpu.roll(c, depth - 1, 1)) for c in center])
            fc, oc, kc = center
            df, do = zero, zero
            for fs, os, ks in sets:
                weight = 0.5 * (kc + ks)
                df = df + weight * (fs - fc)
                do = do + weight * (os - oc)
            prod = fc * oc
            react = r_ref[x, part] * prod / jnp.sqrt(1.0 + prod * prod)
            fn_ref[x, part] = fc + 0.15 * (df - react)
            on_ref[x, part] = oc + 0.15 * (do + react)
    dims = (((0,), (0,)), ((), ()))
    at = 0
    flat = [ref[...].reshape(planes * width, depth) for ref in (fn_ref, on_ref)]
    for a in range(0, depth, LANES):
        total = sum(
            lax.dot_general(u[:, a:a + LANES], u[:, a:], dims, precision=HIGHEST, preferred_element_type=jnp.float32)
            for u in flat
        ) / rows
        for b in range(0, depth - a, LANES):
            g_ref[at:at + LANES] = total[:, b:b + LANES]
            at += LANES


def stencil(n, m, rows, fuel, oxidizer, kappa, rate, halos):
    planes, width, depth = fuel.shape
    blocks = depth // LANES
    field = jax.ShapeDtypeStruct(fuel.shape, jnp.float32)
    vmem = pl.BlockSpec(memory_space=pltpu.VMEM)
    return pl.pallas_call(
        functools.partial(stencil_kernel, n, m, rows, 32),
        out_shape=(field, field, jax.ShapeDtypeStruct((blocks * (blocks + 1) // 2 * LANES, LANES), jnp.float32)),
        in_specs=[vmem] * 8,
        out_specs=(vmem,) * 3,
        name="stencil",
    )(fuel, oxidizer, kappa, rate, *halos)


def sum_kernel(stages, g_ref, out_ref, *scratch):
    count = len(stages)
    inbox, held, sems = scratch[:count], scratch[count:2 * count], scratch[2 * count:]
    index = {"gx": lax.axis_index("gx"), "gy": lax.axis_index("gy")}

    def peer(stage, k):
        axis, stride, size = stage
        mine = lax.rem(index[axis] // stride, size)
        other = lax.rem(mine + k, size)
        place = dict(index)
        place[axis] = index[axis] + (other - mine) * stride
        return mine, other, (place["gx"], place["gy"])

    barrier = pltpu.get_barrier_semaphore()
    greeted = 0
    for stage in stages:
        for k in range(1, stage[2]):
            pl.semaphore_signal(barrier, inc=1, device_id=peer(stage, k)[2], device_id_type=MESH)
            greeted += 1
    pl.semaphore_wait(barrier, greeted)
    source = g_ref
    length = g_ref.shape[0]
    starts = []
    start = 0
    for s, stage in enumerate(stages):
        size = stage[2]
        length //= size
        sent = []
        for k in range(1, size):
            mine, other, device = peer(stage, k)
            sent.append(
                pltpu.make_async_remote_copy(
                    src_ref=source.at[pl.ds(pl.multiple_of(other * length, TILE), length)],
                    dst_ref=inbox[s].at[k - 1],
                    send_sem=sems[0].at[s, k - 1],
                    recv_sem=sems[1].at[s, k - 1],
                    device_id=device,
                    device_id_type=MESH,
                )
            )
            sent[-1].start()
        for copy in sent:
            copy.wait_recv()
        total = source[pl.ds(pl.multiple_of(mine * length, TILE), length)]
        for k in range(1, size):
            total = total + inbox[s][k - 1]
        held[s][...] = total
        for copy in sent:
            copy.wait_send()
        source = held[s]
        start = start + mine * length
        starts.append((start, length))
    part = pl.ds(pl.multiple_of(start, TILE), length)
    out_ref[part] = source[...]
    for s in reversed(range(count)):
        stage = stages[s]
        start, length = starts[s]
        part = pl.ds(pl.multiple_of(start, TILE), length)
        sent = []
        for k in range(1, stage[2]):
            sent.append(
                pltpu.make_async_remote_copy(
                    src_ref=out_ref.at[part],
                    dst_ref=out_ref.at[part],
                    send_sem=sems[2].at[s, k - 1],
                    recv_sem=sems[3].at[s, k - 1],
                    device_id=peer(stage, k)[2],
                    device_id_type=MESH,
                )
            )
            sent[-1].start()
        for copy in sent:
            copy.wait()


def sum_over_all(stages, gram):
    length, lanes = gram.shape
    inbox, held = [], []
    most = max(stage[2] for stage in stages)
    for _, _, size in stages:
        length //= size
        inbox.append(pltpu.VMEM((size - 1, length, lanes), jnp.float32))
        held.append(pltpu.VMEM((length, lanes), jnp.float32))
    vmem = pl.BlockSpec(memory_space=pltpu.VMEM)
    return pl.pallas_call(
        functools.partial(sum_kernel, stages),
        out_shape=jax.ShapeDtypeStruct(gram.shape, jnp.float32),
        in_specs=[vmem],
        out_specs=vmem,
        scratch_shapes=[*inbox, *held] + [pltpu.SemaphoreType.DMA((len(stages), most - 1))] * 4,
        compiler_params=pltpu.CompilerParams(collective_id=1, has_side_effects=True),
        name="allsum",
    )(gram)


def stacked_dot(left, right):
    dims = (((0,), (0,)), ((), ()))
    def pieces(v):
        h = v.astype(jnp.bfloat16).astype(jnp.float32)
        m = (v - h).astype(jnp.bfloat16).astype(jnp.float32)
        return h, m, v - h - m
    (a, b, c), (d, e, f) = pieces(left), pieces(right)
    lhs = jnp.concatenate([a, a, b, a, c, b], axis=0).astype(jnp.bfloat16)
    rhs = jnp.concatenate([d, e, d, f, d, e], axis=0).astype(jnp.bfloat16)
    return lax.dot_general(lhs, rhs, dims, preferred_element_type=jnp.float32)


def column_of(panel, at):
    return jnp.broadcast_to(panel[:, at:at + 1], (TILE, LANES))


def factor_kernel(group, g_ref, r_ref, a_ref):
    depth = r_ref.shape[0]
    blocks = depth // LANES
    at = 0
    for b in range(blocks):
        for c in range(b, blocks):
            a_ref[b * LANES:(b + 1) * LANES, c * LANES:(c + 1) * LANES] = g_ref[at:at + LANES]
            at += LANES
    dims = (((0,), (0,)), ((), ()))
    dot = functools.partial(lax.dot_general, dimension_numbers=dims, precision=HIGHEST, preferred_element_type=jnp.float32)
    sub = lax.broadcasted_iota(jnp.int32, (TILE, LANES), 0)
    lane = lax.broadcasted_iota(jnp.int32, (TILE, LANES), 1)
    for b in range(blocks):
        c0 = b * LANES
        tiles = range(blocks - b)
        if c0:
            r_ref[c0:c0 + LANES, :c0] = jnp.zeros((LANES, c0), jnp.float32)
        for p in range(0, LANES, TILE * group):
            before = []
            for q in range(p, p + TILE * group, TILE):
                r0 = c0 + q
                strips = [a_ref[r0:r0 + TILE, c0 + t * LANES:c0 + (t + 1) * LANES] for t in tiles]
                for s, inv, low, rows in before:
                    factors = []
                    for k in range(TILE):
                        value = column_of(strips[0], s + k)
                        for j in range(k):
                            value = value - factors[j] * low[k, j]
                        factors.append(value * inv[k])
                    for t in tiles:
                        for k in range(TILE):
                            strips[t] = strips[t] - factors[k] * rows[t][k]
                e = {}
                for k in range(TILE):
                    column = column_of(strips[0], q + k)
                    for i in range(k, TILE):
                        e[i, k] = jnp.broadcast_to(column[i:i + 1], (TILE, LANES))
                inv, low = [], {}
                for k in range(TILE):
                    inv.append(lax.rsqrt(e[k, k]))
                    for i in range(k + 1, TILE):
                        low[i, k] = e[i, k] * inv[k]
                    for j in range(k + 1, TILE):
                        for i in range(j, TILE):
                            e[i, j] = e[i, j] - low[i, k] * low[j, k]
                rows = []
                for t in tiles:
                    made = []
                    for k in range(TILE):
                        value = jnp.broadcast_to(strips[t][k:k + 1], (TILE, LANES))
                        for j in range(k):
                            value = value - low[k, j] * made[j]
                        made.append(value * inv[k])
                    rows.append(made)
                    strip = made[0]
                    for k in range(1, TILE):
                        strip = jnp.where(sub == k, made[k], strip)
                    if t == 0:
                        strip = jnp.where(lane >= sub + q, strip, 0.0)
                    r_ref[r0:r0 + TILE, c0 + t * LANES:c0 + (t + 1) * LANES] = strip
                before.append((q, inv, low, rows))
            low_end = p + TILE * group
            if low_end < LANES:
                upper = r_ref[c0 + p:c0 + low_end, c0:]
                a_ref[c0 + low_end:c0 + LANES, c0:] -= stacked_dot(upper[:, :LANES], upper)[low_end:]
        for d in range(b + 1, blocks):
            d0 = d * LANES
            a_ref[d0:d0 + LANES, d0:] -= dot(r_ref[c0:c0 + LANES, d0:d0 + LANES], r_ref[c0:c0 + LANES, d0:])


def factor(gram, depth):
    vmem = pl.BlockSpec(memory_space=pltpu.VMEM)
    return pl.pallas_call(
        functools.partial(factor_kernel, 4),
        out_shape=jax.ShapeDtypeStruct((depth, depth), jnp.float32),
        in_specs=[vmem],
        out_specs=vmem,
        scratch_shapes=[pltpu.VMEM((depth, depth), jnp.float32)],
        name="factor",
    )(gram)


def shards(n, m, fuel, oxidizer, kappa, rate):
    planes, width, depth = fuel.shape
    rows = 2 * planes * width * n * m
    halos = halo(n, m, fuel, oxidizer, kappa)
    fuel_next, oxid_next, gram = stencil(n, m, rows, fuel, oxidizer, kappa, rate, halos)
    pairs = [("gy", 1, 2), ("gy", 2, 2)] if m == 4 else [("gy", 1, m)]
    stages = tuple(pairs + [("gx", 1, n)])
    if gram.shape[0] % (TILE * n * m) == 0:
        gram = sum_over_all(stages, gram)
    else:
        gram = lax.psum(gram, ("gx", "gy"))
    return (fuel_next, oxid_next, factor(gram, depth))


def solution(mesh):
    spec = P("gx", "gy", None)
    body = functools.partial(shards, mesh.shape["gx"], mesh.shape["gy"])
    return jax.shard_map(body, mesh=mesh, in_specs=(spec,) * 4, out_specs=(spec, spec, P()), check_vma=False)
```

```python
import functools

import jax
import jax.numpy as jnp
from jax import lax
from jax.experimental import pallas as pl
from jax.experimental.pallas import tpu as pltpu
from jax.sharding import PartitionSpec as P

MESH = pl.DeviceIdType.MESH
TILE = 8
LANES = 128
HIGHEST = lax.Precision.HIGHEST


def peer(index, stage, k):
    axis, stride, size = stage
    mine = lax.rem(index[axis] // stride, size)
    other = lax.rem(mine + k, size)
    place = dict(index)
    place[axis] = index[axis] + (other - mine) * stride
    return mine, other, (place["gx"], place["gy"])


def sum_over_all(index, stages, source, out_ref, inbox, held, sems):
    count = len(stages)
    length = source.shape[0]
    starts = []
    start = 0
    for s, stage in enumerate(stages):
        size = stage[2]
        length //= size
        sent = []
        for k in range(1, size):
            mine, other, device = peer(index, stage, k)
            sent.append(
                pltpu.make_async_remote_copy(
                    src_ref=source.at[pl.ds(pl.multiple_of(other * length, TILE), length)],
                    dst_ref=inbox[s].at[k - 1],
                    send_sem=sems[0].at[s, k - 1],
                    recv_sem=sems[1].at[s, k - 1],
                    device_id=device,
                    device_id_type=MESH,
                )
            )
            sent[-1].start()
        for copy in sent:
            copy.wait_recv()
        total = source[pl.ds(pl.multiple_of(mine * length, TILE), length)]
        for k in range(1, size):
            total = total + inbox[s][k - 1]
        held[s][...] = total
        for copy in sent:
            copy.wait_send()
        source = held[s]
        start = start + mine * length
        starts.append((start, length))
    part = pl.ds(pl.multiple_of(start, TILE), length)
    out_ref[part] = source[...]
    for s in reversed(range(count)):
        start, length = starts[s]
        part = pl.ds(pl.multiple_of(start, TILE), length)
        sent = []
        for k in range(1, stages[s][2]):
            sent.append(
                pltpu.make_async_remote_copy(
                    src_ref=out_ref.at[part],
                    dst_ref=out_ref.at[part],
                    send_sem=sems[2].at[s, k - 1],
                    recv_sem=sems[3].at[s, k - 1],
                    device_id=peer(index, stages[s], k)[2],
                    device_id_type=MESH,
                )
            )
            sent[-1].start()
        for copy in sent:
            copy.wait()


def update_kernel(
    n, m, rows, parts, stages,
    f_hbm, o_hbm, k_hbm, r_hbm, fn_hbm, on_hbm, g_out,
    f_ref, o_ref, k_ref, r_ref, fn_ref, on_ref, xlo, xhi, ylo, yhi, gram,
    local_sem, xs_sem, xr_sem, ys_sem, yr_sem, *scratch
):
    i, j = lax.axis_index("gx"), lax.axis_index("gy")
    index = {"gx": i, "gy": j}
    planes, width, depth = f_ref.shape
    step = width // parts
    sides = (
        (i < n - 1, i > 0, i + 1, j),
        (i > 0, i < n - 1, i - 1, j),
        (j < m - 1, j > 0, i, j + 1),
        (j > 0, j < m - 1, i, j - 1),
    )
    barrier = pltpu.get_barrier_semaphore()
    greeted = sum(has.astype(jnp.int32) for has, _, _, _ in sides)
    for has, _, a, b in sides:
        @pl.when(has)
        def _(a=a, b=b):
            pl.semaphore_signal(barrier, inc=1, device_id=(a, b), device_id_type=MESH)
    for stage in stages:
        for k in range(1, stage[2]):
            pl.semaphore_signal(barrier, inc=1, device_id=peer(index, stage, k)[2], device_id_type=MESH)
            greeted = greeted + 1
    pl.semaphore_wait(barrier, greeted)
    fields = (f_hbm, o_hbm, k_hbm)

    def x_copies(side, part):
        _, _, a, b = sides[side]
        cut = pl.ds(part * step, step)
        return [
            pltpu.make_async_remote_copy(
                src_ref=ref.at[(planes - 1, 0)[side], cut],
                dst_ref=(xlo, xhi)[side].at[t, cut],
                send_sem=xs_sem.at[side, part, t],
                recv_sem=xr_sem.at[side, part, t],
                device_id=(a, b),
                device_id_type=MESH,
            )
            for t, ref in enumerate(fields)
        ]

    def y_copies(side):
        _, _, a, b = sides[2 + side]
        return [
            pltpu.make_async_remote_copy(
                src_ref=ref.at[:, pl.ds((width - TILE, 0)[side], TILE)],
                dst_ref=(ylo, yhi)[side].at[t],
                send_sem=ys_sem.at[side, t],
                recv_sem=yr_sem.at[side, t],
                device_id=(a, b),
                device_id_type=MESH,
            )
            for t, ref in enumerate(fields)
        ]

    for side in range(2):
        @pl.when(sides[2 + side][0])
        def _(side=side):
            for copy in y_copies(side):
                copy.start()
    for part in range(parts):
        for side in range(2):
            @pl.when(sides[side][0])
            def _(side=side, part=part):
                for copy in x_copies(side, part):
                    copy.start()
    loads = [
        pltpu.make_async_copy(src, dst, local_sem.at[t])
        for t, (src, dst) in enumerate(((f_hbm, f_ref), (o_hbm, o_ref), (k_hbm, k_ref), (r_hbm, r_ref)))
    ]
    for copy in loads:
        copy.start()
    for copy in loads:
        copy.wait()
    for side in range(2):
        @pl.when(sides[2 + side][1])
        def _(side=side):
            for copy in y_copies(side):
                copy.wait_recv()

    row = lax.broadcasted_iota(jnp.int32, (step, depth), 0)
    lane = lax.broadcasted_iota(jnp.int32, (step, depth), 1)
    refs = (f_ref, o_ref, k_ref)
    zero = jnp.zeros((step, depth), jnp.float32)
    zrow = jnp.zeros((1, depth), jnp.float32)
    dims = (((0,), (0,)), ((), ()))
    for q in range(parts):
        for side in range(2):
            @pl.when(sides[side][1])
            def _(side=side, q=q):
                for copy in x_copies(side, q):
                    copy.wait_recv()
        y = q * step
        part = pl.ds(y, step)
        for x in range(planes):
            center = [ref[x, part] for ref in refs]
            sets = []
            if x == 0:
                sets.append([jnp.where(i > 0, xlo[t, part], zero) for t in range(3)])
            else:
                sets.append([ref[x - 1, part] for ref in refs])
            if x == planes - 1:
                sets.append([jnp.where(i < n - 1, xhi[t, part], zero) for t in range(3)])
            else:
                sets.append([ref[x + 1, part] for ref in refs])
            if y == 0:
                before = [jnp.where(j > 0, ylo[t, x, TILE - 1:TILE], zrow) for t in range(3)]
            else:
                before = [ref[x, y - 1:y] for ref in refs]
            if y + step == width:
                after = [jnp.where(j < m - 1, yhi[t, x, 0:1], zrow) for t in range(3)]
            else:
                after = [ref[x, y + step:y + step + 1] for ref in refs]
            sets.append([jnp.where(row == 0, b, pltpu.roll(c, 1, 0)) for b, c in zip(before, center)])
            sets.append([jnp.where(row == step - 1, a, pltpu.roll(c, step - 1, 0)) for a, c in zip(after, center)])
            sets.append([jnp.where(lane == 0, 0.0, pltpu.roll(c, 1, 1)) for c in center])
            sets.append([jnp.where(lane == depth - 1, 0.0, pltpu.roll(c, depth - 1, 1)) for c in center])
            fc, oc, kc = center
            df, do = zero, zero
            for fs, os, ks in sets:
                weight = 0.5 * (kc + ks)
                df = df + weight * (fs - fc)
                do = do + weight * (os - oc)
            prod = fc * oc
            react = r_ref[x, part] * prod / jnp.sqrt(1.0 + prod * prod)
            fn_ref[x, part] = fc + 0.15 * (df - react)
            on_ref[x, part] = oc + 0.15 * (do + react)
        u = jnp.concatenate([ref[x, part] for ref in (fn_ref, on_ref) for x in range(planes)], axis=0)
        at = 0
        for a in range(0, depth, LANES):
            total = lax.dot_general(u[:, a:a + LANES], u[:, a:], dims, precision=HIGHEST, preferred_element_type=jnp.float32)
            for b in range(0, depth - a, LANES):
                block = total[:, b:b + LANES]
                held_rows = slice(at, at + LANES)
                gram[held_rows] = block if q == 0 else gram[held_rows] + block
                at += LANES
    stores = [
        pltpu.make_async_copy(src, dst, local_sem.at[t])
        for t, (src, dst) in enumerate(((fn_ref, fn_hbm), (on_ref, on_hbm)))
    ]
    for copy in stores:
        copy.start()
    gram[...] = gram[...] / rows
    if stages:
        count = len(stages)
        sum_over_all(index, stages, gram, g_out, scratch[:count], scratch[count:2 * count], scratch[2 * count:])
    else:
        g_out[...] = gram[...]
    for side in range(2):
        @pl.when(sides[2 + side][0])
        def _(side=side):
            for copy in y_copies(side):
                copy.wait_send()

        @pl.when(sides[side][0])
        def _(side=side):
            for part in range(parts):
                for copy in x_copies(side, part):
                    copy.wait_send()
    for copy in stores:
        copy.wait()


def update(n, m, rows, stages, fuel, oxidizer, kappa, rate):
    planes, width, depth = fuel.shape
    blocks = depth // LANES
    parts = 4 if width % (4 * TILE) == 0 else 1
    gram_rows = blocks * (blocks + 1) // 2 * LANES
    scratch = [pltpu.VMEM(fuel.shape, jnp.float32)] * 6
    scratch += [pltpu.VMEM((3, width, depth), jnp.float32)] * 2
    scratch += [pltpu.VMEM((3, planes, TILE, depth), jnp.float32)] * 2
    scratch += [pltpu.VMEM((gram_rows, LANES), jnp.float32)]
    scratch += [pltpu.SemaphoreType.DMA((4,))]
    scratch += [pltpu.SemaphoreType.DMA((2, parts, 3))] * 2
    scratch += [pltpu.SemaphoreType.DMA((2, 3))] * 2
    if stages:
        inbox, held, length = [], [], gram_rows
        for _, _, size in stages:
            length //= size
            inbox.append(pltpu.VMEM((size - 1, length, LANES), jnp.float32))
            held.append(pltpu.VMEM((length, LANES), jnp.float32))
        most = max(stage[2] for stage in stages)
        scratch += inbox + held + [pltpu.SemaphoreType.DMA((len(stages), most - 1))] * 4
    field = jax.ShapeDtypeStruct(fuel.shape, jnp.float32)
    any_spec = pl.BlockSpec(memory_space=pl.ANY)
    return pl.pallas_call(
        functools.partial(update_kernel, n, m, rows, parts, stages),
        out_shape=(field, field, jax.ShapeDtypeStruct((gram_rows, LANES), jnp.float32)),
        in_specs=[any_spec] * 4,
        out_specs=(any_spec, any_spec, pl.BlockSpec(memory_space=pltpu.VMEM)),
        scratch_shapes=scratch,
        compiler_params=pltpu.CompilerParams(collective_id=0, has_side_effects=True),
        name="update",
    )(fuel, oxidizer, kappa, rate)


def stacked_dot(left, right):
    dims = (((0,), (0,)), ((), ()))
    def pieces(v):
        h = v.astype(jnp.bfloat16).astype(jnp.float32)
        m = (v - h).astype(jnp.bfloat16).astype(jnp.float32)
        return h, m, v - h - m
    (a, b, c), (d, e, f) = pieces(left), pieces(right)
    lhs = jnp.concatenate([a, a, b, a, c, b], axis=0).astype(jnp.bfloat16)
    rhs = jnp.concatenate([d, e, d, f, d, e], axis=0).astype(jnp.bfloat16)
    return lax.dot_general(lhs, rhs, dims, preferred_element_type=jnp.float32)


def column_of(panel, at):
    return jnp.broadcast_to(panel[:, at:at + 1], (TILE, LANES))


def factor_kernel(group, g_ref, fn_in, on_in, r_ref, fn_out, on_out, a_ref, fn_ref, on_ref, sems):
    loads = [pltpu.make_async_copy(fn_in, fn_ref, sems.at[0]), pltpu.make_async_copy(on_in, on_ref, sems.at[1])]
    stores = [pltpu.make_async_copy(fn_ref, fn_out, sems.at[2]), pltpu.make_async_copy(on_ref, on_out, sems.at[3])]
    for copy in loads:
        copy.start()
    depth = r_ref.shape[0]
    blocks = depth // LANES
    at = 0
    for b in range(blocks):
        for c in range(b, blocks):
            a_ref[b * LANES:(b + 1) * LANES, c * LANES:(c + 1) * LANES] = g_ref[at:at + LANES]
            at += LANES
    dims = (((0,), (0,)), ((), ()))
    dot = functools.partial(lax.dot_general, dimension_numbers=dims, precision=HIGHEST, preferred_element_type=jnp.float32)
    sub = lax.broadcasted_iota(jnp.int32, (TILE, LANES), 0)
    lane = lax.broadcasted_iota(jnp.int32, (TILE, LANES), 1)
    for b in range(blocks):
        c0 = b * LANES
        tiles = range(blocks - b)
        if c0:
            r_ref[c0:c0 + LANES, :c0] = jnp.zeros((LANES, c0), jnp.float32)
        for p in range(0, LANES, TILE * group):
            before = []
            for q in range(p, p + TILE * group, TILE):
                r0 = c0 + q
                strips = [a_ref[r0:r0 + TILE, c0 + t * LANES:c0 + (t + 1) * LANES] for t in tiles]
                for s, inv, low, rows in before:
                    factors = []
                    for k in range(TILE):
                        value = column_of(strips[0], s + k)
                        for j in range(k):
                            value = value - factors[j] * low[k, j]
                        factors.append(value * inv[k])
                    for t in tiles:
                        for k in range(TILE):
                            strips[t] = strips[t] - factors[k] * rows[t][k]
                e = {}
                for k in range(TILE):
                    column = column_of(strips[0], q + k)
                    for i in range(k, TILE):
                        e[i, k] = jnp.broadcast_to(column[i:i + 1], (TILE, LANES))
                inv, low = [], {}
                for k in range(TILE):
                    inv.append(lax.rsqrt(e[k, k]))
                    for i in range(k + 1, TILE):
                        low[i, k] = e[i, k] * inv[k]
                    for j in range(k + 1, TILE):
                        for i in range(j, TILE):
                            e[i, j] = e[i, j] - low[i, k] * low[j, k]
                rows = []
                for t in tiles:
                    made = []
                    for k in range(TILE):
                        value = jnp.broadcast_to(strips[t][k:k + 1], (TILE, LANES))
                        for j in range(k):
                            value = value - low[k, j] * made[j]
                        made.append(value * inv[k])
                    rows.append(made)
                    strip = made[0]
                    for k in range(1, TILE):
                        strip = jnp.where(sub == k, made[k], strip)
                    if t == 0:
                        strip = jnp.where(lane >= sub + q, strip, 0.0)
                    r_ref[r0:r0 + TILE, c0 + t * LANES:c0 + (t + 1) * LANES] = strip
                before.append((q, inv, low, rows))
            low_end = p + TILE * group
            if low_end < LANES:
                upper = r_ref[c0 + p:c0 + low_end, c0:]
                a_ref[c0 + low_end:c0 + LANES, c0:] -= stacked_dot(upper[:, :LANES], upper)[low_end:]
        if b == 0:
            for load, store in zip(loads, stores):
                load.wait()
                store.start()
        for d in range(b + 1, blocks):
            d0 = d * LANES
            a_ref[d0:d0 + LANES, d0:] -= dot(r_ref[c0:c0 + LANES, d0:d0 + LANES], r_ref[c0:c0 + LANES, d0:])
    for copy in stores:
        copy.wait()


def factor(gram, fuel_next, oxid_next):
    depth = fuel_next.shape[2]
    field = jax.ShapeDtypeStruct(fuel_next.shape, jnp.float32)
    vmem = pl.BlockSpec(memory_space=pltpu.VMEM)
    any_spec = pl.BlockSpec(memory_space=pl.ANY)
    return pl.pallas_call(
        functools.partial(factor_kernel, 4),
        out_shape=(jax.ShapeDtypeStruct((depth, depth), jnp.float32), field, field),
        in_specs=[vmem, any_spec, any_spec],
        out_specs=(vmem, any_spec, any_spec),
        scratch_shapes=[
            pltpu.VMEM((depth, depth), jnp.float32),
            pltpu.VMEM(fuel_next.shape, jnp.float32),
            pltpu.VMEM(fuel_next.shape, jnp.float32),
            pltpu.SemaphoreType.DMA((4,)),
        ],
        name="factor",
    )(gram, fuel_next, oxid_next)


def shards(n, m, fuel, oxidizer, kappa, rate):
    planes, width, depth = fuel.shape
    rows = 2 * planes * width * n * m
    blocks = depth // LANES
    stages = ()
    if blocks * (blocks + 1) // 2 * LANES % (TILE * n * m) == 0:
        pairs = [("gy", 1, 2), ("gy", 2, 2)] if m == 4 else [("gy", 1, m)]
        stages = tuple(pairs + [("gx", 1, n)])
    fuel_next, oxid_next, gram = update(n, m, rows, stages, fuel, oxidizer, kappa, rate)
    if not stages:
        gram = lax.psum(gram, ("gx", "gy"))
    r_factor, fuel_next, oxid_next = factor(gram, fuel_next, oxid_next)
    return (fuel_next, oxid_next, r_factor)


def solution(mesh):
    spec = P("gx", "gy", None)
    body = functools.partial(shards, mesh.shape["gx"], mesh.shape["gy"])
    return jax.shard_map(body, mesh=mesh, in_specs=(spec,) * 4, out_specs=(spec, spec, P()), check_vma=False)
```

```python
import functools

import jax
import jax.numpy as jnp
from jax import lax
from jax.experimental import pallas as pl
from jax.experimental.pallas import tpu as pltpu
from jax.sharding import PartitionSpec as P

MESH = pl.DeviceIdType.MESH
TILE = 8
LANES = 128
HIGHEST = lax.Precision.HIGHEST


def peer(index, stage, k):
    axis, stride, size = stage
    mine = lax.rem(index[axis] // stride, size)
    other = lax.rem(mine + k, size)
    place = dict(index)
    place[axis] = index[axis] + (other - mine) * stride
    return mine, other, (place["gx"], place["gy"])


def sum_over_all(index, stages, source, out_ref, inbox, held, sems):
    count = len(stages)
    length = source.shape[0]
    starts = []
    start = 0
    for s, stage in enumerate(stages):
        size = stage[2]
        length //= size
        sent = []
        for k in range(1, size):
            mine, other, device = peer(index, stage, k)
            sent.append(
                pltpu.make_async_remote_copy(
                    src_ref=source.at[pl.ds(pl.multiple_of(other * length, TILE), length)],
                    dst_ref=inbox[s].at[k - 1],
                    send_sem=sems[0].at[s, k - 1],
                    recv_sem=sems[1].at[s, k - 1],
                    device_id=device,
                    device_id_type=MESH,
                )
            )
            sent[-1].start()
        for copy in sent:
            copy.wait_recv()
        total = source[pl.ds(pl.multiple_of(mine * length, TILE), length)]
        for k in range(1, size):
            total = total + inbox[s][k - 1]
        held[s][...] = total
        for copy in sent:
            copy.wait_send()
        source = held[s]
        start = start + mine * length
        starts.append((start, length))
    part = pl.ds(pl.multiple_of(start, TILE), length)
    out_ref[part] = source[...]
    for s in reversed(range(count)):
        start, length = starts[s]
        part = pl.ds(pl.multiple_of(start, TILE), length)
        sent = []
        for k in range(1, stages[s][2]):
            sent.append(
                pltpu.make_async_remote_copy(
                    src_ref=out_ref.at[part],
                    dst_ref=out_ref.at[part],
                    send_sem=sems[2].at[s, k - 1],
                    recv_sem=sems[3].at[s, k - 1],
                    device_id=peer(index, stages[s], k)[2],
                    device_id_type=MESH,
                )
            )
            sent[-1].start()
        for copy in sent:
            copy.wait()


def update_kernel(
    n, m, rows, parts, stages,
    f_hbm, o_hbm, k_hbm, r_hbm, fn_hbm, on_hbm, g_out,
    f_ref, o_ref, k_ref, r_ref, fn_ref, on_ref, xlo, xhi, ylo, yhi, gram, passing,
    local_sem, xs_sem, xr_sem, ys_sem, yr_sem, ps_sem, pr_sem, *scratch
):
    i, j = lax.axis_index("gx"), lax.axis_index("gy")
    index = {"gx": i, "gy": j}
    planes, width, depth = f_ref.shape
    step = width // parts
    sides = (
        (i < n - 1, i > 0, i + 1, j),
        (i > 0, i < n - 1, i - 1, j),
        (j < m - 1, j > 0, i, j + 1),
        (j > 0, j < m - 1, i, j - 1),
    )
    z, odd, depth_z = i // 2, lax.rem(i, 2) == 1, n // 2
    rising = lambda pair: (pair + 1) * parts // depth_z
    falling = lambda pair: (depth_z - 1 - pair) * parts // depth_z
    if n % 2 or n < 4:
        indirect = (0, 0)
        relayed = 0
    else:
        indirect = (jnp.where(odd, falling(z), 0), jnp.where(odd, 0, rising(z - 1)))
        relayed = jnp.where(odd, rising(z - 1), falling(z))
    via = (i - 1, i + 1)
    onward = jnp.where(odd, i - 2, i + 2)
    lands = (jnp.logical_not(odd), odd)
    relayed = jnp.where(odd, jnp.where(z > 0, relayed, 0), jnp.where(z < depth_z - 1, relayed, 0))
    greets = sides + ((i < n - 2, None, i + 2, j), (i > 1, None, i - 2, j))
    barrier = pltpu.get_barrier_semaphore()
    greeted = sum(has.astype(jnp.int32) for has, _, _, _ in greets)
    for has, _, a, b in greets:
        @pl.when(has)
        def _(a=a, b=b):
            pl.semaphore_signal(barrier, inc=1, device_id=(a, b), device_id_type=MESH)
    for stage in stages:
        for k in range(1, stage[2]):
            pl.semaphore_signal(barrier, inc=1, device_id=peer(index, stage, k)[2], device_id_type=MESH)
            greeted = greeted + 1
    pl.semaphore_wait(barrier, greeted)
    fields = (f_hbm, o_hbm, k_hbm)

    def x_copies(side, part):
        _, _, a, b = sides[side]
        cut = pl.ds(part * step, step)
        return [
            pltpu.make_async_remote_copy(
                src_ref=ref.at[(planes - 1, 0)[side], cut],
                dst_ref=(xlo, xhi)[side].at[t, cut],
                send_sem=xs_sem.at[side, part, t],
                recv_sem=xr_sem.at[side, part, t],
                device_id=(a, b),
                device_id_type=MESH,
            )
            for t, ref in enumerate(fields)
        ]

    def to_relay(side, part):
        cut = pl.ds(part * step, step)
        return [
            pltpu.make_async_remote_copy(
                src_ref=ref.at[(planes - 1, 0)[side], cut],
                dst_ref=passing.at[t, cut],
                send_sem=xs_sem.at[side, part, t],
                recv_sem=pr_sem.at[part, t],
                device_id=(via[side], j),
                device_id_type=MESH,
            )
            for t, ref in enumerate(fields)
        ]

    def from_relay(side, part):
        cut = pl.ds(part * step, step)
        return [
            pltpu.make_async_remote_copy(
                src_ref=passing.at[t, cut],
                dst_ref=(xlo, xhi)[side].at[t, cut],
                send_sem=ps_sem.at[part, t],
                recv_sem=xr_sem.at[side, part, t],
                device_id=(onward, j),
                device_id_type=MESH,
            )
            for t in range(3)
        ]

    def y_copies(side):
        _, _, a, b = sides[2 + side]
        return [
            pltpu.make_async_remote_copy(
                src_ref=ref.at[:, pl.ds((width - TILE, 0)[side], TILE)],
                dst_ref=(ylo, yhi)[side].at[t],
                send_sem=ys_sem.at[side, t],
                recv_sem=yr_sem.at[side, t],
                device_id=(a, b),
                device_id_type=MESH,
            )
            for t, ref in enumerate(fields)
        ]

    for side in range(2):
        @pl.when(sides[2 + side][0])
        def _(side=side):
            for copy in y_copies(side):
                copy.start()
    for part in range(parts):
        for side in range(2):
            @pl.when(sides[side][0] & (part >= indirect[side]))
            def _(side=side, part=part):
                for copy in x_copies(side, part):
                    copy.start()

            @pl.when(sides[side][0] & (part < indirect[side]))
            def _(side=side, part=part):
                for copy in to_relay(side, part):
                    copy.start()
    loads = [
        pltpu.make_async_copy(src, dst, local_sem.at[t])
        for t, (src, dst) in enumerate(((f_hbm, f_ref), (o_hbm, o_ref), (k_hbm, k_ref), (r_hbm, r_ref)))
    ]
    for copy in loads:
        copy.start()
    for copy in loads:
        copy.wait()
    for side in range(2):
        @pl.when(sides[2 + side][1])
        def _(side=side):
            for copy in y_copies(side):
                copy.wait_recv()

    row = lax.broadcasted_iota(jnp.int32, (step, depth), 0)
    lane = lax.broadcasted_iota(jnp.int32, (step, depth), 1)
    refs = (f_ref, o_ref, k_ref)
    zero = jnp.zeros((step, depth), jnp.float32)
    zrow = jnp.zeros((1, depth), jnp.float32)
    dims = (((0,), (0,)), ((), ()))
    for q in range(parts):
        @pl.when(q < relayed)
        def _(q=q):
            for copy in to_relay(0, q):
                copy.wait_recv()

        for side in range(2):
            @pl.when((q < relayed) & lands[side])
            def _(side=side, q=q):
                for copy in from_relay(side, q):
                    copy.start()

        for side in range(2):
            @pl.when(sides[side][1])
            def _(side=side, q=q):
                for copy in x_copies(side, q):
                    copy.wait_recv()
        y = q * step
        part = pl.ds(y, step)
        for x in range(planes):
            center = [ref[x, part] for ref in refs]
            sets = []
            if x == 0:
                sets.append([jnp.where(i > 0, xlo[t, part], zero) for t in range(3)])
            else:
                sets.append([ref[x - 1, part] for ref in refs])
            if x == planes - 1:
                sets.append([jnp.where(i < n - 1, xhi[t, part], zero) for t in range(3)])
            else:
                sets.append([ref[x + 1, part] for ref in refs])
            if y == 0:
                before = [jnp.where(j > 0, ylo[t, x, TILE - 1:TILE], zrow) for t in range(3)]
            else:
                before = [ref[x, y - 1:y] for ref in refs]
            if y + step == width:
                after = [jnp.where(j < m - 1, yhi[t, x, 0:1], zrow) for t in range(3)]
            else:
                after = [ref[x, y + step:y + step + 1] for ref in refs]
            sets.append([jnp.where(row == 0, b, pltpu.roll(c, 1, 0)) for b, c in zip(before, center)])
            sets.append([jnp.where(row == step - 1, a, pltpu.roll(c, step - 1, 0)) for a, c in zip(after, center)])
            sets.append([jnp.where(lane == 0, 0.0, pltpu.roll(c, 1, 1)) for c in center])
            sets.append([jnp.where(lane == depth - 1, 0.0, pltpu.roll(c, depth - 1, 1)) for c in center])
            fc, oc, kc = center
            df, do = zero, zero
            for fs, os, ks in sets:
                weight = 0.5 * (kc + ks)
                df = df + weight * (fs - fc)
                do = do + weight * (os - oc)
            prod = fc * oc
            react = r_ref[x, part] * prod / jnp.sqrt(1.0 + prod * prod)
            fn_ref[x, part] = fc + 0.15 * (df - react)
            on_ref[x, part] = oc + 0.15 * (do + react)
        u = jnp.concatenate([ref[x, part] for ref in (fn_ref, on_ref) for x in range(planes)], axis=0)
        at = 0
        for a in range(0, depth, LANES):
            total = lax.dot_general(u[:, a:a + LANES], u[:, a:], dims, precision=HIGHEST, preferred_element_type=jnp.float32)
            for b in range(0, depth - a, LANES):
                block = total[:, b:b + LANES]
                held_rows = slice(at, at + LANES)
                gram[held_rows] = block if q == 0 else gram[held_rows] + block
                at += LANES
    stores = [
        pltpu.make_async_copy(src, dst, local_sem.at[t])
        for t, (src, dst) in enumerate(((fn_ref, fn_hbm), (on_ref, on_hbm)))
    ]
    for copy in stores:
        copy.start()
    gram[...] = gram[...] / rows
    if stages:
        count = len(stages)
        sum_over_all(index, stages, gram, g_out, scratch[:count], scratch[count:2 * count], scratch[2 * count:])
    else:
        g_out[...] = gram[...]
    for side in range(2):
        @pl.when(sides[2 + side][0])
        def _(side=side):
            for copy in y_copies(side):
                copy.wait_send()

        @pl.when(sides[side][0])
        def _(side=side):
            for part in range(parts):
                for copy in x_copies(side, part):
                    copy.wait_send()

    for part in range(parts):
        @pl.when(part < relayed)
        def _(part=part):
            for copy in from_relay(0, part):
                copy.wait_send()
    for copy in stores:
        copy.wait()


def update(n, m, rows, stages, fuel, oxidizer, kappa, rate):
    planes, width, depth = fuel.shape
    blocks = depth // LANES
    parts = 4 if width % (4 * TILE) == 0 else 1
    gram_rows = blocks * (blocks + 1) // 2 * LANES
    scratch = [pltpu.VMEM(fuel.shape, jnp.float32)] * 6
    scratch += [pltpu.VMEM((3, width, depth), jnp.float32)] * 2
    scratch += [pltpu.VMEM((3, planes, TILE, depth), jnp.float32)] * 2
    scratch += [pltpu.VMEM((gram_rows, LANES), jnp.float32)]
    scratch += [pltpu.VMEM((3, width, depth), jnp.float32)]
    scratch += [pltpu.SemaphoreType.DMA((4,))]
    scratch += [pltpu.SemaphoreType.DMA((2, parts, 3))] * 2
    scratch += [pltpu.SemaphoreType.DMA((2, 3))] * 2
    scratch += [pltpu.SemaphoreType.DMA((parts, 3))] * 2
    if stages:
        inbox, held, length = [], [], gram_rows
        for _, _, size in stages:
            length //= size
            inbox.append(pltpu.VMEM((size - 1, length, LANES), jnp.float32))
            held.append(pltpu.VMEM((length, LANES), jnp.float32))
        most = max(stage[2] for stage in stages)
        scratch += inbox + held + [pltpu.SemaphoreType.DMA((len(stages), most - 1))] * 4
    field = jax.ShapeDtypeStruct(fuel.shape, jnp.float32)
    any_spec = pl.BlockSpec(memory_space=pl.ANY)
    return pl.pallas_call(
        functools.partial(update_kernel, n, m, rows, parts, stages),
        out_shape=(field, field, jax.ShapeDtypeStruct((gram_rows, LANES), jnp.float32)),
        in_specs=[any_spec] * 4,
        out_specs=(any_spec, any_spec, pl.BlockSpec(memory_space=pltpu.VMEM)),
        scratch_shapes=scratch,
        compiler_params=pltpu.CompilerParams(collective_id=0, has_side_effects=True),
        name="update",
    )(fuel, oxidizer, kappa, rate)


def stacked_dot(left, right):
    dims = (((0,), (0,)), ((), ()))
    def pieces(v):
        h = v.astype(jnp.bfloat16).astype(jnp.float32)
        m = (v - h).astype(jnp.bfloat16).astype(jnp.float32)
        return h, m, v - h - m
    (a, b, c), (d, e, f) = pieces(left), pieces(right)
    lhs = jnp.concatenate([a, a, b, a, c, b], axis=0).astype(jnp.bfloat16)
    rhs = jnp.concatenate([d, e, d, f, d, e], axis=0).astype(jnp.bfloat16)
    return lax.dot_general(lhs, rhs, dims, preferred_element_type=jnp.float32)


def column_of(panel, at):
    return jnp.broadcast_to(panel[:, at:at + 1], (TILE, LANES))


def factor_kernel(group, g_ref, fn_in, on_in, r_ref, fn_out, on_out, a_ref, fn_ref, on_ref, sems):
    loads = [pltpu.make_async_copy(fn_in, fn_ref, sems.at[0]), pltpu.make_async_copy(on_in, on_ref, sems.at[1])]
    stores = [pltpu.make_async_copy(fn_ref, fn_out, sems.at[2]), pltpu.make_async_copy(on_ref, on_out, sems.at[3])]
    for copy in loads:
        copy.start()
    depth = r_ref.shape[0]
    blocks = depth // LANES
    at = 0
    for b in range(blocks):
        for c in range(b, blocks):
            a_ref[b * LANES:(b + 1) * LANES, c * LANES:(c + 1) * LANES] = g_ref[at:at + LANES]
            at += LANES
    dims = (((0,), (0,)), ((), ()))
    dot = functools.partial(lax.dot_general, dimension_numbers=dims, precision=HIGHEST, preferred_element_type=jnp.float32)
    sub = lax.broadcasted_iota(jnp.int32, (TILE, LANES), 0)
    lane = lax.broadcasted_iota(jnp.int32, (TILE, LANES), 1)
    for b in range(blocks):
        c0 = b * LANES
        tiles = range(blocks - b)
        if c0:
            r_ref[c0:c0 + LANES, :c0] = jnp.zeros((LANES, c0), jnp.float32)
        for p in range(0, LANES, TILE * group):
            before = []
            for q in range(p, p + TILE * group, TILE):
                r0 = c0 + q
                strips = [a_ref[r0:r0 + TILE, c0 + t * LANES:c0 + (t + 1) * LANES] for t in tiles]
                for s, inv, low, rows in before:
                    factors = []
                    for k in range(TILE):
                        value = column_of(strips[0], s + k)
                        for j in range(k):
                            value = value - factors[j] * low[k, j]
                        factors.append(value * inv[k])
                    for t in tiles:
                        for k in range(TILE):
                            strips[t] = strips[t] - factors[k] * rows[t][k]
                e = {}
                for k in range(TILE):
                    column = column_of(strips[0], q + k)
                    for i in range(k, TILE):
                        e[i, k] = jnp.broadcast_to(column[i:i + 1], (TILE, LANES))
                inv, low = [], {}
                for k in range(TILE):
                    inv.append(lax.rsqrt(e[k, k]))
                    for i in range(k + 1, TILE):
                        low[i, k] = e[i, k] * inv[k]
                    for j in range(k + 1, TILE):
                        for i in range(j, TILE):
                            e[i, j] = e[i, j] - low[i, k] * low[j, k]
                rows = []
                for t in tiles:
                    made = []
                    for k in range(TILE):
                        value = jnp.broadcast_to(strips[t][k:k + 1], (TILE, LANES))
                        for j in range(k):
                            value = value - low[k, j] * made[j]
                        made.append(value * inv[k])
                    rows.append(made)
                    strip = made[0]
                    for k in range(1, TILE):
                        strip = jnp.where(sub == k, made[k], strip)
                    if t == 0:
                        strip = jnp.where(lane >= sub + q, strip, 0.0)
                    r_ref[r0:r0 + TILE, c0 + t * LANES:c0 + (t + 1) * LANES] = strip
                before.append((q, inv, low, rows))
            low_end = p + TILE * group
            if low_end < LANES:
                upper = r_ref[c0 + p:c0 + low_end, c0:]
                a_ref[c0 + low_end:c0 + LANES, c0:] -= stacked_dot(upper[:, :LANES], upper)[low_end:]
        if b == 0:
            for load, store in zip(loads, stores):
                load.wait()
                store.start()
        for d in range(b + 1, blocks):
            d0 = d * LANES
            a_ref[d0:d0 + LANES, d0:] -= dot(r_ref[c0:c0 + LANES, d0:d0 + LANES], r_ref[c0:c0 + LANES, d0:])
    for copy in stores:
        copy.wait()


def factor(gram, fuel_next, oxid_next):
    depth = fuel_next.shape[2]
    field = jax.ShapeDtypeStruct(fuel_next.shape, jnp.float32)
    vmem = pl.BlockSpec(memory_space=pltpu.VMEM)
    any_spec = pl.BlockSpec(memory_space=pl.ANY)
    return pl.pallas_call(
        functools.partial(factor_kernel, 4),
        out_shape=(jax.ShapeDtypeStruct((depth, depth), jnp.float32), field, field),
        in_specs=[vmem, any_spec, any_spec],
        out_specs=(vmem, any_spec, any_spec),
        scratch_shapes=[
            pltpu.VMEM((depth, depth), jnp.float32),
            pltpu.VMEM(fuel_next.shape, jnp.float32),
            pltpu.VMEM(fuel_next.shape, jnp.float32),
            pltpu.SemaphoreType.DMA((4,)),
        ],
        name="factor",
    )(gram, fuel_next, oxid_next)


def shards(n, m, fuel, oxidizer, kappa, rate):
    planes, width, depth = fuel.shape
    rows = 2 * planes * width * n * m
    blocks = depth // LANES
    stages = ()
    if blocks * (blocks + 1) // 2 * LANES % (TILE * n * m) == 0:
        pairs = [("gy", 1, 2), ("gy", 2, 2)] if m == 4 else [("gy", 1, m)]
        stages = tuple(pairs + [("gx", 1, n)])
    fuel_next, oxid_next, gram = update(n, m, rows, stages, fuel, oxidizer, kappa, rate)
    if not stages:
        gram = lax.psum(gram, ("gx", "gy"))
    r_factor, fuel_next, oxid_next = factor(gram, fuel_next, oxid_next)
    return (fuel_next, oxid_next, r_factor)


def solution(mesh):
    spec = P("gx", "gy", None)
    body = functools.partial(shards, mesh.shape["gx"], mesh.shape["gy"])
    return jax.shard_map(body, mesh=mesh, in_specs=(spec,) * 4, out_specs=(spec, spec, P()), check_vma=False)
```

```python
import functools

import jax
import jax.numpy as jnp
from jax import lax
from jax.experimental import pallas as pl
from jax.experimental.pallas import tpu as pltpu
from jax.sharding import PartitionSpec as P

MESH = pl.DeviceIdType.MESH
TILE = 8
LANES = 128
HIGHEST = lax.Precision.HIGHEST


def peer(index, stage, k):
    axis, stride, size = stage
    mine = lax.rem(index[axis] // stride, size)
    other = lax.rem(mine + k, size)
    place = dict(index)
    place[axis] = index[axis] + (other - mine) * stride
    return mine, other, (place["gx"], place["gy"])


def sum_over_all(index, stages, source, out_ref, inbox, held, sems):
    count = len(stages)
    length = source.shape[0]
    starts = []
    start = 0
    for s, stage in enumerate(stages):
        size = stage[2]
        length //= size
        sent = []
        for k in range(1, size):
            mine, other, device = peer(index, stage, k)
            sent.append(
                pltpu.make_async_remote_copy(
                    src_ref=source.at[pl.ds(pl.multiple_of(other * length, TILE), length)],
                    dst_ref=inbox[s].at[k - 1],
                    send_sem=sems[0].at[s, k - 1],
                    recv_sem=sems[1].at[s, k - 1],
                    device_id=device,
                    device_id_type=MESH,
                )
            )
            sent[-1].start()
        for copy in sent:
            copy.wait_recv()
        total = source[pl.ds(pl.multiple_of(mine * length, TILE), length)]
        for k in range(1, size):
            total = total + inbox[s][k - 1]
        held[s][...] = total
        for copy in sent:
            copy.wait_send()
        source = held[s]
        start = start + mine * length
        starts.append((start, length))
    part = pl.ds(pl.multiple_of(start, TILE), length)
    out_ref[part] = source[...]
    for s in reversed(range(count)):
        start, length = starts[s]
        part = pl.ds(pl.multiple_of(start, TILE), length)
        sent = []
        for k in range(1, stages[s][2]):
            sent.append(
                pltpu.make_async_remote_copy(
                    src_ref=out_ref.at[part],
                    dst_ref=out_ref.at[part],
                    send_sem=sems[2].at[s, k - 1],
                    recv_sem=sems[3].at[s, k - 1],
                    device_id=peer(index, stages[s], k)[2],
                    device_id_type=MESH,
                )
            )
            sent[-1].start()
        for copy in sent:
            copy.wait()


def update_kernel(
    n, m, rows, parts, stages,
    f_hbm, o_hbm, k_hbm, r_hbm, fn_hbm, on_hbm, g_out,
    f_ref, o_ref, k_ref, r_ref, fn_ref, on_ref, xlo, xhi, ylo, yhi, gram, passing,
    local_sem, xs_sem, xr_sem, ys_sem, yr_sem, ps_sem, pr_sem, *scratch
):
    i, j = lax.axis_index("gx"), lax.axis_index("gy")
    index = {"gx": i, "gy": j}
    planes, width, depth = f_ref.shape
    step = width // parts
    sides = (
        (i < n - 1, i > 0, i + 1, j),
        (i > 0, i < n - 1, i - 1, j),
        (j < m - 1, j > 0, i, j + 1),
        (j > 0, j < m - 1, i, j - 1),
    )
    z, odd, depth_z = i // 2, lax.rem(i, 2) == 1, n // 2
    rising = lambda pair: (pair + 1) * parts // depth_z
    falling = lambda pair: (depth_z - 1 - pair) * parts // depth_z
    if n % 2 or n < 4:
        indirect = (0, 0)
        relayed = 0
    else:
        indirect = (jnp.where(odd, falling(z), 0), jnp.where(odd, 0, rising(z - 1)))
        relayed = jnp.where(odd, rising(z - 1), falling(z))
    via = (i - 1, i + 1)
    onward = jnp.where(odd, i - 2, i + 2)
    lands = (jnp.logical_not(odd), odd)
    relayed = jnp.where(odd, jnp.where(z > 0, relayed, 0), jnp.where(z < depth_z - 1, relayed, 0))
    greets = sides + ((i < n - 2, None, i + 2, j), (i > 1, None, i - 2, j))
    barrier = pltpu.get_barrier_semaphore()
    greeted = sum(has.astype(jnp.int32) for has, _, _, _ in greets)
    for has, _, a, b in greets:
        @pl.when(has)
        def _(a=a, b=b):
            pl.semaphore_signal(barrier, inc=1, device_id=(a, b), device_id_type=MESH)
    for stage in stages:
        for k in range(1, stage[2]):
            pl.semaphore_signal(barrier, inc=1, device_id=peer(index, stage, k)[2], device_id_type=MESH)
            greeted = greeted + 1
    pl.semaphore_wait(barrier, greeted)
    fields = (f_hbm, o_hbm, k_hbm)

    def x_copies(side, part):
        _, _, a, b = sides[side]
        cut = pl.ds(part * step, step)
        return [
            pltpu.make_async_remote_copy(
                src_ref=ref.at[(planes - 1, 0)[side], cut],
                dst_ref=(xlo, xhi)[side].at[t, cut],
                send_sem=xs_sem.at[side, part, t],
                recv_sem=xr_sem.at[side, part, t],
                device_id=(a, b),
                device_id_type=MESH,
            )
            for t, ref in enumerate(fields)
        ]

    def to_relay(side, part):
        cut = pl.ds(part * step, step)
        return [
            pltpu.make_async_remote_copy(
                src_ref=ref.at[(planes - 1, 0)[side], cut],
                dst_ref=passing.at[t, cut],
                send_sem=xs_sem.at[side, part, t],
                recv_sem=pr_sem.at[part, t],
                device_id=(via[side], j),
                device_id_type=MESH,
            )
            for t, ref in enumerate(fields)
        ]

    def from_relay(side, part):
        cut = pl.ds(part * step, step)
        return [
            pltpu.make_async_remote_copy(
                src_ref=passing.at[t, cut],
                dst_ref=(xlo, xhi)[side].at[t, cut],
                send_sem=ps_sem.at[part, t],
                recv_sem=xr_sem.at[side, part, t],
                device_id=(onward, j),
                device_id_type=MESH,
            )
            for t in range(3)
        ]

    def y_copies(side):
        _, _, a, b = sides[2 + side]
        return [
            pltpu.make_async_remote_copy(
                src_ref=ref.at[:, pl.ds((width - TILE, 0)[side], TILE)],
                dst_ref=(ylo, yhi)[side].at[t],
                send_sem=ys_sem.at[side, t],
                recv_sem=yr_sem.at[side, t],
                device_id=(a, b),
                device_id_type=MESH,
            )
            for t, ref in enumerate(fields)
        ]

    for side in range(2):
        @pl.when(sides[2 + side][0])
        def _(side=side):
            for copy in y_copies(side):
                copy.start()
    for part in range(parts):
        for side in range(2):
            @pl.when(sides[side][0] & (part >= indirect[side]))
            def _(side=side, part=part):
                for copy in x_copies(side, part):
                    copy.start()

            @pl.when(sides[side][0] & (part < indirect[side]))
            def _(side=side, part=part):
                for copy in to_relay(side, part):
                    copy.start()
    loads = [
        pltpu.make_async_copy(src, dst, local_sem.at[t])
        for t, (src, dst) in enumerate(((f_hbm, f_ref), (o_hbm, o_ref), (k_hbm, k_ref), (r_hbm, r_ref)))
    ]
    for copy in loads:
        copy.start()
    for copy in loads:
        copy.wait()
    for side in range(2):
        @pl.when(sides[2 + side][1])
        def _(side=side):
            for copy in y_copies(side):
                copy.wait_recv()

    row = lax.broadcasted_iota(jnp.int32, (step, depth), 0)
    lane = lax.broadcasted_iota(jnp.int32, (step, depth), 1)
    refs = (f_ref, o_ref, k_ref)
    zero = jnp.zeros((step, depth), jnp.float32)
    zrow = jnp.zeros((1, depth), jnp.float32)
    dims = (((0,), (0,)), ((), ()))
    for q in range(parts):
        @pl.when(q < relayed)
        def _(q=q):
            for copy in to_relay(0, q):
                copy.wait_recv()

        for side in range(2):
            @pl.when((q < relayed) & lands[side])
            def _(side=side, q=q):
                for copy in from_relay(side, q):
                    copy.start()

        for side in range(2):
            @pl.when(sides[side][1])
            def _(side=side, q=q):
                for copy in x_copies(side, q):
                    copy.wait_recv()
        y = q * step
        part = pl.ds(y, step)
        for x in range(planes):
            center = [ref[x, part] for ref in refs]
            sets = []
            if x == 0:
                sets.append([jnp.where(i > 0, xlo[t, part], zero) for t in range(3)])
            else:
                sets.append([ref[x - 1, part] for ref in refs])
            if x == planes - 1:
                sets.append([jnp.where(i < n - 1, xhi[t, part], zero) for t in range(3)])
            else:
                sets.append([ref[x + 1, part] for ref in refs])
            if y == 0:
                before = [jnp.where(j > 0, ylo[t, x, TILE - 1:TILE], zrow) for t in range(3)]
            else:
                before = [ref[x, y - 1:y] for ref in refs]
            if y + step == width:
                after = [jnp.where(j < m - 1, yhi[t, x, 0:1], zrow) for t in range(3)]
            else:
                after = [ref[x, y + step:y + step + 1] for ref in refs]
            sets.append([jnp.where(row == 0, b, pltpu.roll(c, 1, 0)) for b, c in zip(before, center)])
            sets.append([jnp.where(row == step - 1, a, pltpu.roll(c, step - 1, 0)) for a, c in zip(after, center)])
            sets.append([jnp.where(lane == 0, 0.0, pltpu.roll(c, 1, 1)) for c in center])
            sets.append([jnp.where(lane == depth - 1, 0.0, pltpu.roll(c, depth - 1, 1)) for c in center])
            fc, oc, kc = center
            df, do = zero, zero
            for fs, os, ks in sets:
                weight = 0.5 * (kc + ks)
                df = df + weight * (fs - fc)
                do = do + weight * (os - oc)
            prod = fc * oc
            react = r_ref[x, part] * prod / jnp.sqrt(1.0 + prod * prod)
            fn_ref[x, part] = fc + 0.15 * (df - react)
            on_ref[x, part] = oc + 0.15 * (do + react)
        u = jnp.concatenate([ref[x, part] for ref in (fn_ref, on_ref) for x in range(planes)], axis=0)
        at = 0
        for a in range(0, depth, LANES):
            total = lax.dot_general(u[:, a:a + LANES], u[:, a:], dims, precision=HIGHEST, preferred_element_type=jnp.float32)
            for b in range(0, depth - a, LANES):
                block = total[:, b:b + LANES]
                held_rows = slice(at, at + LANES)
                gram[held_rows] = block if q == 0 else gram[held_rows] + block
                at += LANES
    stores = [
        pltpu.make_async_copy(src, dst, local_sem.at[t])
        for t, (src, dst) in enumerate(((fn_ref, fn_hbm), (on_ref, on_hbm)))
    ]
    for copy in stores:
        copy.start()
    gram[...] = gram[...] / rows
    if stages:
        count = len(stages)
        sum_over_all(index, stages, gram, g_out, scratch[:count], scratch[count:2 * count], scratch[2 * count:])
    else:
        g_out[...] = gram[...]
    for side in range(2):
        @pl.when(sides[2 + side][0])
        def _(side=side):
            for copy in y_copies(side):
                copy.wait_send()

        @pl.when(sides[side][0])
        def _(side=side):
            for part in range(parts):
                for copy in x_copies(side, part):
                    copy.wait_send()

    for part in range(parts):
        @pl.when(part < relayed)
        def _(part=part):
            for copy in from_relay(0, part):
                copy.wait_send()
    for copy in stores:
        copy.wait()


def update(n, m, rows, stages, fuel, oxidizer, kappa, rate):
    planes, width, depth = fuel.shape
    blocks = depth // LANES
    parts = 8 if width % (8 * TILE) == 0 else 1
    gram_rows = blocks * (blocks + 1) // 2 * LANES
    scratch = [pltpu.VMEM(fuel.shape, jnp.float32)] * 6
    scratch += [pltpu.VMEM((3, width, depth), jnp.float32)] * 2
    scratch += [pltpu.VMEM((3, planes, TILE, depth), jnp.float32)] * 2
    scratch += [pltpu.VMEM((gram_rows, LANES), jnp.float32)]
    scratch += [pltpu.VMEM((3, width, depth), jnp.float32)]
    scratch += [pltpu.SemaphoreType.DMA((4,))]
    scratch += [pltpu.SemaphoreType.DMA((2, parts, 3))] * 2
    scratch += [pltpu.SemaphoreType.DMA((2, 3))] * 2
    scratch += [pltpu.SemaphoreType.DMA((parts, 3))] * 2
    if stages:
        inbox, held, length = [], [], gram_rows
        for _, _, size in stages:
            length //= size
            inbox.append(pltpu.VMEM((size - 1, length, LANES), jnp.float32))
            held.append(pltpu.VMEM((length, LANES), jnp.float32))
        most = max(stage[2] for stage in stages)
        scratch += inbox + held + [pltpu.SemaphoreType.DMA((len(stages), most - 1))] * 4
    field = jax.ShapeDtypeStruct(fuel.shape, jnp.float32)
    any_spec = pl.BlockSpec(memory_space=pl.ANY)
    return pl.pallas_call(
        functools.partial(update_kernel, n, m, rows, parts, stages),
        out_shape=(field, field, jax.ShapeDtypeStruct((gram_rows, LANES), jnp.float32)),
        in_specs=[any_spec] * 4,
        out_specs=(any_spec, any_spec, pl.BlockSpec(memory_space=pltpu.VMEM)),
        scratch_shapes=scratch,
        compiler_params=pltpu.CompilerParams(collective_id=0, has_side_effects=True),
        name="update",
    )(fuel, oxidizer, kappa, rate)


def stacked_dot(left, right):
    dims = (((0,), (0,)), ((), ()))
    def pieces(v):
        h = v.astype(jnp.bfloat16).astype(jnp.float32)
        m = (v - h).astype(jnp.bfloat16).astype(jnp.float32)
        return h, m, v - h - m
    (a, b, c), (d, e, f) = pieces(left), pieces(right)
    lhs = jnp.concatenate([a, a, b, a, c, b], axis=0).astype(jnp.bfloat16)
    rhs = jnp.concatenate([d, e, d, f, d, e], axis=0).astype(jnp.bfloat16)
    return lax.dot_general(lhs, rhs, dims, preferred_element_type=jnp.float32)


def column_of(panel, at):
    return jnp.broadcast_to(panel[:, at:at + 1], (TILE, LANES))


def factor_kernel(group, g_ref, fn_in, on_in, r_ref, fn_out, on_out, a_ref, fn_ref, on_ref, sems):
    loads = [pltpu.make_async_copy(fn_in, fn_ref, sems.at[0]), pltpu.make_async_copy(on_in, on_ref, sems.at[1])]
    stores = [pltpu.make_async_copy(fn_ref, fn_out, sems.at[2]), pltpu.make_async_copy(on_ref, on_out, sems.at[3])]
    for copy in loads:
        copy.start()
    depth = r_ref.shape[0]
    blocks = depth // LANES
    at = 0
    for b in range(blocks):
        for c in range(b, blocks):
            a_ref[b * LANES:(b + 1) * LANES, c * LANES:(c + 1) * LANES] = g_ref[at:at + LANES]
            at += LANES
    dims = (((0,), (0,)), ((), ()))
    dot = functools.partial(lax.dot_general, dimension_numbers=dims, precision=HIGHEST, preferred_element_type=jnp.float32)
    sub = lax.broadcasted_iota(jnp.int32, (TILE, LANES), 0)
    lane = lax.broadcasted_iota(jnp.int32, (TILE, LANES), 1)
    for b in range(blocks):
        c0 = b * LANES
        tiles = range(blocks - b)
        if c0:
            r_ref[c0:c0 + LANES, :c0] = jnp.zeros((LANES, c0), jnp.float32)
        for p in range(0, LANES, TILE * group):
            before = []
            for q in range(p, p + TILE * group, TILE):
                r0 = c0 + q
                strips = [a_ref[r0:r0 + TILE, c0 + t * LANES:c0 + (t + 1) * LANES] for t in tiles]
                for s, inv, low, rows in before:
                    factors = []
                    for k in range(TILE):
                        value = column_of(strips[0], s + k)
                        for j in range(k):
                            value = value - factors[j] * low[k, j]
                        factors.append(value * inv[k])
                    for t in tiles:
                        for k in range(TILE):
                            strips[t] = strips[t] - factors[k] * rows[t][k]
                e = {}
                for k in range(TILE):
                    column = column_of(strips[0], q + k)
                    for i in range(k, TILE):
                        e[i, k] = jnp.broadcast_to(column[i:i + 1], (TILE, LANES))
                inv, low = [], {}
                for k in range(TILE):
                    inv.append(lax.rsqrt(e[k, k]))
                    for i in range(k + 1, TILE):
                        low[i, k] = e[i, k] * inv[k]
                    for j in range(k + 1, TILE):
                        for i in range(j, TILE):
                            e[i, j] = e[i, j] - low[i, k] * low[j, k]
                rows = []
                for t in tiles:
                    made = []
                    for k in range(TILE):
                        value = jnp.broadcast_to(strips[t][k:k + 1], (TILE, LANES))
                        for j in range(k):
                            value = value - low[k, j] * made[j]
                        made.append(value * inv[k])
                    rows.append(made)
                    strip = made[0]
                    for k in range(1, TILE):
                        strip = jnp.where(sub == k, made[k], strip)
                    if t == 0:
                        strip = jnp.where(lane >= sub + q, strip, 0.0)
                    r_ref[r0:r0 + TILE, c0 + t * LANES:c0 + (t + 1) * LANES] = strip
                before.append((q, inv, low, rows))
            low_end = p + TILE * group
            if low_end < LANES:
                upper = r_ref[c0 + p:c0 + low_end, c0:]
                a_ref[c0 + low_end:c0 + LANES, c0:] -= stacked_dot(upper[:, :LANES], upper)[low_end:]
        if b == 0:
            for load, store in zip(loads, stores):
                load.wait()
                store.start()
        for d in range(b + 1, blocks):
            d0 = d * LANES
            a_ref[d0:d0 + LANES, d0:] -= dot(r_ref[c0:c0 + LANES, d0:d0 + LANES], r_ref[c0:c0 + LANES, d0:])
    for copy in stores:
        copy.wait()


def factor(gram, fuel_next, oxid_next):
    depth = fuel_next.shape[2]
    field = jax.ShapeDtypeStruct(fuel_next.shape, jnp.float32)
    vmem = pl.BlockSpec(memory_space=pltpu.VMEM)
    any_spec = pl.BlockSpec(memory_space=pl.ANY)
    return pl.pallas_call(
        functools.partial(factor_kernel, 4),
        out_shape=(jax.ShapeDtypeStruct((depth, depth), jnp.float32), field, field),
        in_specs=[vmem, any_spec, any_spec],
        out_specs=(vmem, any_spec, any_spec),
        scratch_shapes=[
            pltpu.VMEM((depth, depth), jnp.float32),
            pltpu.VMEM(fuel_next.shape, jnp.float32),
            pltpu.VMEM(fuel_next.shape, jnp.float32),
            pltpu.SemaphoreType.DMA((4,)),
        ],
        name="factor",
    )(gram, fuel_next, oxid_next)


def shards(n, m, fuel, oxidizer, kappa, rate):
    planes, width, depth = fuel.shape
    rows = 2 * planes * width * n * m
    blocks = depth // LANES
    stages = ()
    if blocks * (blocks + 1) // 2 * LANES % (TILE * n * m) == 0:
        pairs = [("gy", 1, 2), ("gy", 2, 2)] if m == 4 else [("gy", 1, m)]
        stages = tuple(pairs + [("gx", 1, n)])
    fuel_next, oxid_next, gram = update(n, m, rows, stages, fuel, oxidizer, kappa, rate)
    if not stages:
        gram = lax.psum(gram, ("gx", "gy"))
    r_factor, fuel_next, oxid_next = factor(gram, fuel_next, oxid_next)
    return (fuel_next, oxid_next, r_factor)


def solution(mesh):
    spec = P("gx", "gy", None)
    body = functools.partial(shards, mesh.shape["gx"], mesh.shape["gy"])
    return jax.shard_map(body, mesh=mesh, in_specs=(spec,) * 4, out_specs=(spec, spec, P()), check_vma=False)
```
